256 devices in a mesh: dp: 16 (over z_lo, x, core), tensor: 16 (over y, z_hi).
Axes of the slice: x: 4, y: 4, z: 8 (z_hi: 4, z_lo: 2; z = z_hi * 2 + z_lo), core: 2. Of those that a mesh axis runs over, the one named last changes fastest.
Arguments:
- tokens: bfloat16 [16384, 4096], P(('dp', 'tensor')), parts along dimension 0, may hold values from -6 to 6
- gate_rows: int32 [224, 9], P('tensor'), may hold values from -1 to 31, as said below
- gate_blocks: bfloat16 [224, 9, 128, 128], P('tensor'), may hold values from -0.21875 to 0.21875
- up_rows: int32 [224, 9], P('tensor'), may hold values from -1 to 31, as said below
- up_blocks: bfloat16 [224, 9, 128, 128], P('tensor'), may hold values from -0.21875 to 0.21875
Outputs:
- hidden: bfloat16 [16384, 28672], P('dp', 'tensor'), parts along dimension 0
The draws below stay inside these ranges and needn't reach their ends.
There are 16 independent parts, one for each index of `dp`. The reference program is written for one: setup_inputs(seed, part) draws one part's arguments, and reference() takes and returns one part's arrays. A program takes and returns all parts, laid end to end along the dimension named above; an argument that names none is the same for every part. Nothing has to cross between parts.
Inputs may be any that keep to these rules, and one draw needn't show every extreme that they name: `gate_rows`: row c lists, for block column c of 128 hidden units, the row blocks of its nonzero blocks, all different, followed by -1 in the unused slots; every tensor member's 14 block columns include one with exactly 9 entries. `up_rows`: as for gate_rows, drawn apart.
All inputs are finite; a program needn't handle non-finite values.
Results may differ from the reference program's by a relative error of at most 0.001.
Values may be sent and summed in bfloat16 or wider, within the bound.
No kernel may reach another device: no remote copies, remote signals or barrier semaphores. Data moves between devices by JAX's collectives and lax.ppermute only.
A program may use at most 192 MiB of HBM per device.

```python
import jax
import jax.numpy as jnp
from jax import lax

D = 4096
FF = 28672
BLK = 128
CAP = 9
TOKENS = 1024
ROWBLK = 32
COLBLK = 14
SLOTS = 224
N_TENSOR = 16


def block_rows_common(key, salt_value):
    base_key = jax.random.fold_in(key, salt_value)
    first_key, second_key, third_key = jax.random.split(base_key, 3)
    line_count = N_TENSOR * COLBLK
    counts = jax.random.randint(first_key, (line_count,), CAP // 3, CAP + 1)
    chosen = jax.random.randint(second_key, (N_TENSOR,), 0, COLBLK)
    full_line = jnp.arange(line_count) % COLBLK == jnp.repeat(chosen, COLBLK)
    counts = jnp.where(full_line, CAP, counts)
    orders = jax.vmap(lambda one_key: jax.random.permutation(one_key, ROWBLK))(jax.random.split(third_key, line_count))
    orders = orders[:, :CAP]
    kept = jnp.arange(CAP)[None, :] < counts[:, None]
    return jnp.where(kept, orders, -1).astype(jnp.int32)


def draw_gate_rows(key, part):
    return block_rows_common(key, 11)


def draw_up_rows(key, part):
    return block_rows_common(key, 23)


def block_levels(key, shape, cuts, least, high):
    gain = 1.0
    for dim, blocks in cuts:
        heights = jax.random.uniform(jax.random.fold_in(jax.random.fold_in(key, 6), dim), (blocks,), jnp.float32, least / len(cuts), high / len(cuts))
        gain = gain * jnp.repeat(jnp.exp(heights), shape[dim] // blocks).reshape((-1,) + (1,) * (len(shape) - 1 - dim))
    return gain


def normal_values(key, shape, scale, most, cuts=(), dtype=jnp.bfloat16):
    values = scale * jax.random.normal(key, shape, jnp.float32)
    if cuts:
        values = values * block_levels(key, shape, cuts, -0.22, 0.18)
    return jnp.clip(values, -most, most).astype(dtype)


def setup_inputs(seed: int = 0, part: int = 0) -> dict:
    streams_of = jax.random.split(jax.random.key(seed), 6)
    part_splits = jax.random.split(jax.random.fold_in(streams_of[5], part), 6)
    return {
        "tokens": normal_values(part_splits[0], (TOKENS, D), 1.0, 6.0, ((0, 16),)),
        "gate_rows": draw_gate_rows(jax.random.fold_in(streams_of[5], 71), part),
        "gate_blocks": normal_values(streams_of[2], (SLOTS, CAP, BLK, BLK), (CAP * BLK * 2 // 3) ** -0.5, 0.21875, ((0, 16),)),
        "up_rows": draw_up_rows(jax.random.fold_in(streams_of[5], 71), part),
        "up_blocks": normal_values(streams_of[4], (SLOTS, CAP, BLK, BLK), (CAP * BLK * 2 // 3) ** -0.5, 0.21875, ((0, 16),)),
    }


def member_columns(tokens, row_list, block_values):
    row_total = tokens.shape[0]
    col_blocks = row_list.shape[0]
    capacity = row_list.shape[1]
    block_size = block_values.shape[-1]
    token_blocks = tokens.astype(jnp.float32).reshape(row_total, -1, block_size)
    flat_index = jnp.maximum(row_list, 0).reshape(-1).astype(jnp.int32)
    picked = jnp.take(token_blocks, flat_index, axis=1).reshape(row_total, col_blocks, capacity, block_size)
    picked = jnp.where((row_list >= 0)[None, :, :, None], picked, jnp.zeros((), jnp.float32))
    summed = jnp.einsum("rcjk,cjkn->rcn", picked, block_values.astype(jnp.float32))
    return summed.reshape(row_total, col_blocks * block_size)


def reference(tokens, gate_rows, gate_blocks, up_rows, up_blocks):
    members = N_TENSOR
    gate_list = gate_rows.reshape(members, COLBLK, CAP)
    up_list = up_rows.reshape(members, COLBLK, CAP)
    gate_vals = gate_blocks.reshape(members, COLBLK, CAP, BLK, BLK)
    up_vals = up_blocks.reshape(members, COLBLK, CAP, BLK, BLK)

    def one_member(operands):
        gate_part = member_columns(tokens, operands[0], operands[1])
        up_part = member_columns(tokens, operands[2], operands[3])
        return (jax.nn.silu(gate_part) * up_part).astype(jnp.bfloat16)

    stacked = lax.map(one_member, (gate_list, gate_vals, up_list, up_vals))
    return jnp.transpose(stacked, (1, 0, 2)).reshape(TOKENS, FF)
```

```python
import functools

import jax
import jax.numpy as jnp
import numpy as np
from jax import lax
from jax.experimental import pallas as pl
from jax.experimental.pallas import tpu as pltpu
from jax.sharding import PartitionSpec as P

BLK = 128
SIDE = 4
AXES = ("dp", "tensor")
TURNED = 16
UNROLL = 7
COST = 22_000_000


def moved(member, core, dim, step):
    y, z = member // SIDE, member % SIDE
    v = y if dim == "y" else z
    v = v ^ 1 if (step + core) % 2 == 0 else SIDE - 1 - v
    return v * SIDE + z if dim == "y" else y * SIDE + v


class Piece:
    def __init__(self, rows, sources, size, offset):
        self.rows, self.sources, self.size, self.offset = rows, sources, size, offset

    def part(self, offset, size):
        count = self.rows.shape[0] // self.size
        rows = self.rows.reshape(count, self.size, -1)[:, offset : offset + size]
        return Piece(rows.reshape(count * size, -1), self.sources, size, self.offset + offset)


def joined(*pieces):
    rows = jnp.concatenate([p.rows for p in pieces], axis=0)
    return Piece(rows, lambda m, core: [s for p in pieces for s in p.sources(m, core)], pieces[0].size, pieces[0].offset)


def project_kernel(layout, first_block, n_prev, dst_ref, gate_rows_ref, up_rows_ref, *refs):
    n = len(layout)
    pieces, (gate_ref, up_ref) = refs[:n], refs[n : n + 2]
    out_ref, hidden, sems = refs[n + 2 + n_prev :]
    columns, cap = gate_rows_ref.shape

    def product(rows_ref, blocks_ref, c):
        def gathered(j):
            start = pl.multiple_of(jnp.maximum(rows_ref[c, j], 0) * BLK, BLK)
            return jnp.concatenate([p[:, pl.ds(start, BLK)] for p in pieces], axis=0)

        lhs = jnp.concatenate([gathered(j) for j in range(cap)], axis=1)
        rhs = jnp.concatenate(
            [jnp.where(rows_ref[c, j] >= 0, blocks_ref[c, j], jnp.zeros((), blocks_ref.dtype)) for j in range(cap)], axis=0
        )
        return jnp.dot(lhs, rhs, preferred_element_type=jnp.float32)

    @pl.loop(0, columns, step=UNROLL)
    def _(first):
        for k in range(UNROLL):
            c = first + k
            gate = product(gate_rows_ref, gate_ref, c)
            up = product(up_rows_ref, up_ref, c)
            value = gate * (1.0 / (1.0 + jnp.exp(-gate))) * up
            hidden[:, pl.ds(pl.multiple_of(c * BLK, BLK), BLK)] = value.astype(hidden.dtype)

    copies, base = [], 0
    for size, count in layout:
        for _ in range(count):
            i = len(copies)
            to = pl.multiple_of(dst_ref[first_block + i], 16)
            copies.append(pltpu.make_async_copy(hidden.at[pl.ds(base, size)], out_ref.at[pl.ds(to, size)], sems.at[i]))
            base += size
    for copy in copies:
        copy.start()
    for copy in copies:
        copy.wait()


def project(pieces, total_rows, dst, first_block, tables, blocks, result):
    rows = sum(p.rows.shape[0] for p in pieces)
    layout = [(p.size, p.rows.shape[0] // p.size) for p in pieces]
    width = blocks[0].shape[0] * BLK
    prev = [] if result is None else [result]
    vmem, smem, hbm = (pl.BlockSpec(memory_space=m) for m in (pltpu.VMEM, pltpu.SMEM, pl.ANY))
    cap = tables[0].shape[1]
    return pl.pallas_call(
        functools.partial(project_kernel, layout, first_block, len(prev)),
        out_shape=jax.ShapeDtypeStruct((total_rows, width), jnp.bfloat16),
        in_specs=[smem] * 3 + [vmem] * (len(pieces) + 2) + [hbm] * len(prev),
        out_specs=hbm,
        scratch_shapes=[
            pltpu.VMEM((rows, width), jnp.bfloat16),
            pltpu.SemaphoreType.DMA((sum(count for _, count in layout),)),
        ],
        input_output_aliases={5 + len(pieces): 0} if prev else {},
        cost_estimate=pl.CostEstimate(
            flops=COST * (rows + 110), bytes_accessed=2 * rows * width, transcendentals=rows * width
        ),
        compiler_params=pltpu.CompilerParams(vmem_limit_bytes=8 << 20),
    )(dst, *tables, *[p.rows for p in pieces], *blocks, *prev)


def solution(mesh):
    groups, members = mesh.shape["dp"], mesh.shape["tensor"]

    def swap(piece, dim, step):
        pairs = [
            (g * members + m, g * members + moved(m, g % 2, dim, step)) for g in range(groups) for m in range(members)
        ]
        rows = lax.ppermute(piece.rows, AXES, pairs)
        return Piece(
            rows, lambda m, core: piece.sources(moved(m, core, dim, step), core), piece.size, piece.offset
        )

    def shards(tokens, gate_rows, gate_blocks, up_rows, up_blocks):
        local = tokens.shape[0]
        blocks = (gate_blocks, up_blocks)
        tables = (gate_rows, up_rows)

        own = Piece(tokens, lambda m, core: [m], local, 0)
        mine = own.part(TURNED, local - TURNED)
        z1 = swap(mine, "z", 0)
        y1 = swap(own, "y", 0)
        z2 = swap(joined(mine, z1), "z", 1)
        y2 = swap(joined(own, y1), "y", 1)
        p1 = swap(z1, "y", 0)
        p2 = swap(joined(z1, p1), "y", 1)
        column = joined(own.part(0, TURNED), y1.part(0, TURNED), y2.part(0, TURNED))
        b1 = swap(column, "z", 0)
        q1 = swap(z2, "y", 0)
        b2 = swap(joined(column, b1), "z", 1)
        q2 = swap(joined(z2, q1), "y", 1)
        calls = ([own], [z1, y1], [y2, p1], [z2, p2], [q1, b1], [b2], [q2])
        places = np.array(
            [
                [
                    [s * local + p.offset for pieces in calls for p in pieces for s in p.sources(m, core)]
                    for m in range(members)
                ]
                for core in range(2)
            ],
            np.int32,
        )
        dst = jnp.asarray(places)[lax.axis_index("dp") % 2, lax.axis_index("tensor")]
        out, first = None, 0
        for pieces in calls:
            out = project(pieces, members * local, dst, first, tables, blocks, out)
            first += sum(p.rows.shape[0] // p.size for p in pieces)
        return out

    in_specs = (
        P(AXES, None),
        P("tensor", None),
        P("tensor", None, None, None),
        P("tensor", None),
        P("tensor", None, None, None),
    )
    return jax.shard_map(shards, mesh=mesh, in_specs=in_specs, out_specs=P("dp", "tensor"), check_vma=False)
```

```python
import functools

import jax
import jax.numpy as jnp
import numpy as np
from jax import lax
from jax.experimental import pallas as pl
from jax.experimental.pallas import tpu as pltpu
from jax.sharding import PartitionSpec as P

BLK = 128
SIDE = 4
AXES = ("dp", "tensor")
TURNED = 16
UNROLL = 7
COST = 22_000_000


STEPS = {("y", 0): 1, ("y", 1): 2, ("z", 0): 4, ("z", 1): 8}


def mask(core, code):
    found = 0
    for (dim, step), bit in STEPS.items():
        if code & bit:
            found ^= (1, 3)[(step + core) % 2] * (SIDE if dim == "y" else 1)
    return found


class Piece:
    def __init__(self, rows, codes, size, offset):
        self.rows, self.codes, self.size, self.offset = rows, codes, size, offset

    def part(self, offset, size):
        rows = self.rows.reshape(len(self.codes), self.size, -1)[:, offset : offset + size]
        return Piece(rows.reshape(len(self.codes) * size, -1), self.codes, size, self.offset + offset)


def joined(*pieces):
    rows = jnp.concatenate([p.rows for p in pieces], axis=0)
    return Piece(rows, sum([p.codes for p in pieces], []), pieces[0].size, pieces[0].offset)


def after(piece, *others):
    rows, *_ = lax.optimization_barrier((piece.rows, *[getattr(o, "rows", o) for o in others]))
    return Piece(rows, piece.codes, piece.size, piece.offset)


def project_kernel(layout, starts, n_prev, table_ref, *refs):
    n = len(layout)
    pieces, (gate_ref, up_ref) = refs[:n], refs[n : n + 2]
    out_ref, hidden, sems = refs[n + 2 + n_prev :]
    columns, cap = gate_ref.shape[:2]

    def product(start, blocks_ref, c):
        listed = [table_ref[start + c * cap + j] for j in range(cap)]

        def gathered(j):
            start = pl.multiple_of(jnp.maximum(listed[j], 0) * BLK, BLK)
            return jnp.concatenate([p[:, pl.ds(start, BLK)] for p in pieces], axis=0)

        lhs = jnp.concatenate([gathered(j) for j in range(cap)], axis=1)
        rhs = jnp.concatenate(
            [jnp.where(listed[j] >= 0, blocks_ref[c, j], jnp.zeros((), blocks_ref.dtype)) for j in range(cap)], axis=0
        )
        return jnp.dot(lhs, rhs, preferred_element_type=jnp.float32)

    @pl.loop(0, columns, step=UNROLL)
    def _(first):
        for k in range(UNROLL):
            c = first + k
            gate = product(starts[0], gate_ref, c)
            up = product(starts[1], up_ref, c)
            value = gate * (1.0 / (1.0 + jnp.exp(-gate))) * up
            hidden[:, pl.ds(pl.multiple_of(c * BLK, BLK), BLK)] = value.astype(hidden.dtype)

    copies, base = [], 0
    for codes, size, offset in layout:
        for code in codes:
            i = len(copies)
            to = pl.multiple_of(table_ref[code] + offset, 16)
            copies.append(pltpu.make_async_copy(hidden.at[pl.ds(base, size)], out_ref.at[pl.ds(to, size)], sems.at[i]))
            base += size
    for copy in copies:
        copy.start()
    for copy in copies:
        copy.wait()


def project(pieces, total_rows, table, starts, blocks, result):
    rows = sum(p.rows.shape[0] for p in pieces)
    layout = [(p.codes, p.size, p.offset) for p in pieces]
    width = blocks[0].shape[0] * BLK
    prev = [] if result is None else [result]
    vmem, smem, hbm = (pl.BlockSpec(memory_space=m) for m in (pltpu.VMEM, pltpu.SMEM, pl.ANY))
    return pl.pallas_call(
        functools.partial(project_kernel, layout, starts, len(prev)),
        out_shape=jax.ShapeDtypeStruct((total_rows, width), jnp.bfloat16),
        in_specs=[smem] + [vmem] * (len(pieces) + 2) + [hbm] * len(prev),
        out_specs=hbm,
        scratch_shapes=[
            pltpu.VMEM((rows, width), jnp.bfloat16),
            pltpu.SemaphoreType.DMA((sum(len(p.codes) for p in pieces),)),
        ],
        input_output_aliases={3 + len(pieces): 0} if prev else {},
        cost_estimate=pl.CostEstimate(
            flops=COST * (rows + 110), bytes_accessed=2 * rows * width, transcendentals=rows * width
        ),
        compiler_params=pltpu.CompilerParams(vmem_limit_bytes=8 << 20),
    )(table, *[p.rows for p in pieces], *blocks, *prev)


def solution(mesh):
    groups, members = mesh.shape["dp"], mesh.shape["tensor"]

    def swap(piece, dim, step):
        bit = STEPS[dim, step]
        pairs = [(g * members + m, g * members + (m ^ mask(g % 2, bit))) for g in range(groups) for m in range(members)]
        rows = lax.ppermute(piece.rows, AXES, pairs)
        return Piece(rows, [code ^ bit for code in piece.codes], piece.size, piece.offset)

    def shards(tokens, gate_rows, gate_blocks, up_rows, up_blocks):
        local = tokens.shape[0]
        masks = jnp.asarray(np.array([[mask(core, code) for code in range(members)] for core in range(2)], np.int32))
        core, me = lax.axis_index("dp") % 2, lax.axis_index("tensor")
        table = jnp.concatenate([(masks[core] ^ me) * local, gate_rows.reshape(-1), up_rows.reshape(-1)])
        starts = (members, members + gate_rows.size)
        run = lambda pieces, result: project(
            pieces, members * local, table, starts, (gate_blocks, up_blocks), result
        )

        own = Piece(tokens, [0], local, 0)
        mine = own.part(TURNED, local - TURNED)
        z1 = swap(mine, "z", 0)
        y1 = swap(own, "y", 0)
        y2 = swap(own, "y", 1)
        z2 = swap(mine, "z", 1)
        y3 = swap(y1, "y", 1)
        result = run([own, y1], None)
        z1, z2 = after(z1, result), after(z2, result)
        z3 = swap(after(z1, y3), "z", 1)
        pair = joined(z1, z2)
        p1 = swap(after(pair, y3), "y", 0)
        column = joined(*[p.part(0, TURNED) for p in (own, y1, y2, y3)])
        b1 = swap(column, "z", 0)
        b2 = swap(column, "z", 1)
        q1 = swap(after(z3, p1), "y", 0)
        p2 = swap(joined(pair, p1), "y", 1)
        b3 = swap(b1, "z", 1)
        q2 = swap(after(joined(z3, q1), b1), "y", 1)
        for pieces in ([y2, z1, z2], [y3, z3, p1], [q1, b1, b2], [p2], [b3], [q2]):
            result = run(pieces, result)
        return result

    in_specs = (
        P(AXES, None),
        P("tensor", None),
        P("tensor", None, None, None),
        P("tensor", None),
        P("tensor", None, None, None),
    )
    return jax.shard_map(shards, mesh=mesh, in_specs=in_specs, out_specs=P("dp", "tensor"), check_vma=False)
```

```python
import functools

import jax
import jax.numpy as jnp
import numpy as np
from jax import lax
from jax.experimental import pallas as pl
from jax.experimental.pallas import tpu as pltpu
from jax.sharding import PartitionSpec as P

BLK = 128
SIDE = 4
AXES = ("dp", "tensor")
TURNED = 16
UNROLL = 7
COST = 22_000_000


STEPS = {("y", 0): 1, ("y", 1): 2, ("z", 0): 4, ("z", 1): 8}


def mask(core, code):
    found = 0
    for (dim, step), bit in STEPS.items():
        if code & bit:
            found ^= (1, 3)[(step + core) % 2] * (SIDE if dim == "y" else 1)
    return found


class Piece:
    def __init__(self, rows, codes, size, offset):
        self.rows, self.codes, self.size, self.offset = rows, codes, size, offset

    def part(self, offset, size):
        rows = self.rows.reshape(len(self.codes), self.size, -1)[:, offset : offset + size]
        return Piece(rows.reshape(len(self.codes) * size, -1), self.codes, size, self.offset + offset)


def joined(*pieces):
    rows = jnp.concatenate([p.rows for p in pieces], axis=0)
    return Piece(rows, sum([p.codes for p in pieces], []), pieces[0].size, pieces[0].offset)


def after(piece, *others):
    rows, *_ = lax.optimization_barrier((piece.rows, *[getattr(o, "rows", o) for o in others]))
    return Piece(rows, piece.codes, piece.size, piece.offset)


def project_kernel(layout, starts, n_prev, table_ref, *refs):
    n = len(layout)
    pieces, (gate_ref, up_ref) = refs[:n], refs[n : n + 2]
    out_ref, hidden, sems = refs[n + 2 + n_prev :]
    columns, cap = gate_ref.shape[:2]

    def product(start, blocks_ref, c):
        listed = [table_ref[start + c * cap + j] for j in range(cap)]

        def gathered(j):
            start = pl.multiple_of(jnp.maximum(listed[j], 0) * BLK, BLK)
            return jnp.concatenate([p[:, pl.ds(start, BLK)] for p in pieces], axis=0)

        lhs = jnp.concatenate([gathered(j) for j in range(cap)], axis=1)
        rhs = jnp.concatenate(
            [jnp.where(listed[j] >= 0, blocks_ref[c, j], jnp.zeros((), blocks_ref.dtype)) for j in range(cap)], axis=0
        )
        return jnp.dot(lhs, rhs, preferred_element_type=jnp.float32)

    @pl.loop(0, columns, step=UNROLL)
    def _(first):
        for k in range(UNROLL):
            c = first + k
            gate = product(starts[0], gate_ref, c)
            up = product(starts[1], up_ref, c)
            value = gate * (1.0 / (1.0 + jnp.exp(-gate))) * up
            hidden[:, pl.ds(pl.multiple_of(c * BLK, BLK), BLK)] = value.astype(hidden.dtype)

    copies, base = [], 0
    for codes, size, offset in layout:
        for code in codes:
            i = len(copies)
            to = pl.multiple_of(table_ref[code] + offset, 16)
            copies.append(pltpu.make_async_copy(hidden.at[pl.ds(base, size)], out_ref.at[pl.ds(to, size)], sems.at[i]))
            base += size
    for copy in copies:
        copy.start()
    for copy in copies:
        copy.wait()


def project(pieces, total_rows, table, starts, blocks, result):
    rows = sum(p.rows.shape[0] for p in pieces)
    layout = [(p.codes, p.size, p.offset) for p in pieces]
    width = blocks[0].shape[0] * BLK
    prev = [] if result is None else [result]
    vmem, smem, hbm = (pl.BlockSpec(memory_space=m) for m in (pltpu.VMEM, pltpu.SMEM, pl.ANY))
    return pl.pallas_call(
        functools.partial(project_kernel, layout, starts, len(prev)),
        out_shape=jax.ShapeDtypeStruct((total_rows, width), jnp.bfloat16),
        in_specs=[smem] + [vmem] * (len(pieces) + 2) + [hbm] * len(prev),
        out_specs=hbm,
        scratch_shapes=[
            pltpu.VMEM((rows, width), jnp.bfloat16),
            pltpu.SemaphoreType.DMA((sum(len(p.codes) for p in pieces),)),
        ],
        input_output_aliases={3 + len(pieces): 0} if prev else {},
        cost_estimate=pl.CostEstimate(
            flops=COST * (rows + 110), bytes_accessed=2 * rows * width, transcendentals=rows * width
        ),
        compiler_params=pltpu.CompilerParams(vmem_limit_bytes=8 << 20),
    )(table, *[p.rows for p in pieces], *blocks, *prev)


def solution(mesh):
    groups, members = mesh.shape["dp"], mesh.shape["tensor"]

    def swap(piece, dim, step):
        bit = STEPS[dim, step]
        pairs = [(g * members + m, g * members + (m ^ mask(g % 2, bit))) for g in range(groups) for m in range(members)]
        rows = lax.ppermute(piece.rows, AXES, pairs)
        return Piece(rows, [code ^ bit for code in piece.codes], piece.size, piece.offset)

    def shards(tokens, gate_rows, gate_blocks, up_rows, up_blocks):
        local = tokens.shape[0]
        masks = jnp.asarray(np.array([[mask(core, code) for code in range(members)] for core in range(2)], np.int32))
        core, me = lax.axis_index("dp") % 2, lax.axis_index("tensor")
        table = jnp.concatenate([(masks[core] ^ me) * local, gate_rows.reshape(-1), up_rows.reshape(-1)])
        starts = (members, members + gate_rows.size)
        run = lambda pieces, result: project(
            pieces, members * local, table, starts, (gate_blocks, up_blocks), result
        )

        own = Piece(tokens, [0], local, 0)
        mine = own.part(TURNED, local - TURNED)
        y1 = swap(own, "y", 0)
        y2 = swap(own, "y", 1)
        z1 = swap(mine, "z", 0)
        z2 = swap(mine, "z", 1)
        y3 = swap(y1, "y", 1)
        z1, z2 = after(z1, y1, y2), after(z2, y1, y2)
        z3 = swap(after(z1, y3), "z", 1)
        pair = joined(z1, z2)
        p1 = swap(after(pair, y3), "y", 0)
        column = joined(*[p.part(0, TURNED) for p in (own, y1, y2, y3)])
        b1 = swap(column, "z", 0)
        p2 = swap(joined(pair, p1), "y", 1)
        q1 = swap(after(z3, p1), "y", 0)
        b2 = swap(after(column, z3), "z", 1)
        b3 = swap(after(b1, q1), "z", 1)
        q2 = swap(after(joined(z3, q1), b1), "y", 1)
        result = None
        for pieces in ([own, y1, after(y2, y3)], [y3, z1, z2], [z3, p1, b1], [q1, p2], [b2, b3], [q2]):
            result = run(pieces, result)
        return result

    in_specs = (
        P(AXES, None),
        P("tensor", None),
        P("tensor", None, None, None),
        P("tensor", None),
        P("tensor", None, None, None),
    )
    return jax.shard_map(shards, mesh=mesh, in_specs=in_specs, out_specs=P("dp", "tensor"), check_vma=False)
```

```python
import functools

import jax
import jax.numpy as jnp
import numpy as np
from jax import lax
from jax.experimental import pallas as pl
from jax.experimental.pallas import tpu as pltpu
from jax.sharding import PartitionSpec as P

BLK = 128
SIDE = 4
AXES = ("dp", "tensor")
TURNED = 16
UNROLL = 7
COST = 30_000_000


STEPS = {("y", 0): 1, ("y", 1): 2, ("z", 0): 4, ("z", 1): 8}


def mask(core, code):
    found = 0
    for (dim, step), bit in STEPS.items():
        if code & bit:
            found ^= (1, 3)[(step + core) % 2] * (SIDE if dim == "y" else 1)
    return found


class Piece:
    def __init__(self, rows, codes, size, offset):
        self.rows, self.codes, self.size, self.offset = rows, codes, size, offset

    def part(self, offset, size):
        rows = self.rows.reshape(len(self.codes), self.size, -1)[:, offset : offset + size]
        return Piece(rows.reshape(len(self.codes) * size, -1), self.codes, size, self.offset + offset)


def joined(*pieces):
    rows = jnp.concatenate([p.rows for p in pieces], axis=0)
    return Piece(rows, sum([p.codes for p in pieces], []), pieces[0].size, pieces[0].offset)


def after(piece, *others):
    rows, *_ = lax.optimization_barrier((piece.rows, *[getattr(o, "rows", o) for o in others]))
    return Piece(rows, piece.codes, piece.size, piece.offset)


def met_kernel(table_ref, *refs):
    refs[-1][...] = table_ref[...]


def met(table, *arrays):
    vmem = pl.BlockSpec(memory_space=pltpu.VMEM)
    return pl.pallas_call(
        met_kernel,
        out_shape=jax.ShapeDtypeStruct(table.shape, table.dtype),
        in_specs=[vmem] * (1 + len(arrays)),
        out_specs=vmem,
        compiler_params=pltpu.CompilerParams(vmem_limit_bytes=1 << 20),
    )(table, *arrays)


def project_kernel(layout, starts, n_prev, table_ref, *refs):
    n = len(layout)
    pieces, (gate_ref, up_ref) = refs[:n], refs[n : n + 2]
    out_ref, hidden, sems = refs[n + 2 + n_prev :]
    columns, cap = gate_ref.shape[:2]

    def product(start, blocks_ref, c):
        listed = [table_ref[start + c * cap + j] for j in range(cap)]

        def gathered(j):
            start = pl.multiple_of(jnp.maximum(listed[j], 0) * BLK, BLK)
            return jnp.concatenate([p[:, pl.ds(start, BLK)] for p in pieces], axis=0)

        lhs = jnp.concatenate([gathered(j) for j in range(cap)], axis=1)
        rhs = jnp.concatenate(
            [jnp.where(listed[j] >= 0, blocks_ref[c, j], jnp.zeros((), blocks_ref.dtype)) for j in range(cap)], axis=0
        )
        return jnp.dot(lhs, rhs, preferred_element_type=jnp.float32)

    @pl.loop(0, columns, step=UNROLL)
    def _(first):
        for k in range(UNROLL):
            c = first + k
            gate = product(starts[0], gate_ref, c)
            up = product(starts[1], up_ref, c)
            value = gate * (1.0 / (1.0 + jnp.exp(-gate))) * up
            hidden[:, pl.ds(pl.multiple_of(c * BLK, BLK), BLK)] = value.astype(hidden.dtype)

    copies, base = [], 0
    for codes, size, offset in layout:
        for code in codes:
            i = len(copies)
            to = pl.multiple_of(table_ref[code] + offset, 16)
            copies.append(pltpu.make_async_copy(hidden.at[pl.ds(base, size)], out_ref.at[pl.ds(to, size)], sems.at[i]))
            base += size
    for copy in copies:
        copy.start()
    for copy in copies:
        copy.wait()


def project(pieces, total_rows, table, starts, blocks, result):
    rows = sum(p.rows.shape[0] for p in pieces)
    layout = [(p.codes, p.size, p.offset) for p in pieces]
    width = blocks[0].shape[0] * BLK
    prev = [] if result is None else [result]
    vmem, smem, hbm = (pl.BlockSpec(memory_space=m) for m in (pltpu.VMEM, pltpu.SMEM, pl.ANY))
    return pl.pallas_call(
        functools.partial(project_kernel, layout, starts, len(prev)),
        out_shape=jax.ShapeDtypeStruct((total_rows, width), jnp.bfloat16),
        in_specs=[smem] + [vmem] * (len(pieces) + 2) + [hbm] * len(prev),
        out_specs=hbm,
        scratch_shapes=[
            pltpu.VMEM((rows, width), jnp.bfloat16),
            pltpu.SemaphoreType.DMA((sum(len(p.codes) for p in pieces),)),
        ],
        input_output_aliases={3 + len(pieces): 0} if prev else {},
        cost_estimate=pl.CostEstimate(
            flops=COST * (rows + 110), bytes_accessed=2 * rows * width, transcendentals=rows * width
        ),
        compiler_params=pltpu.CompilerParams(vmem_limit_bytes=8 << 20),
    )(table, *[p.rows for p in pieces], *blocks, *prev)


def solution(mesh):
    groups, members = mesh.shape["dp"], mesh.shape["tensor"]

    def swap(piece, dim, step):
        bit = STEPS[dim, step]
        pairs = [(g * members + m, g * members + (m ^ mask(g % 2, bit))) for g in range(groups) for m in range(members)]
        rows = lax.ppermute(piece.rows, AXES, pairs)
        return Piece(rows, [code ^ bit for code in piece.codes], piece.size, piece.offset)

    def shards(tokens, gate_rows, gate_blocks, up_rows, up_blocks):
        local = tokens.shape[0]
        masks = jnp.asarray(np.array([[mask(core, code) for code in range(members)] for core in range(2)], np.int32))
        core, me = lax.axis_index("dp") % 2, lax.axis_index("tensor")
        table = jnp.concatenate([(masks[core] ^ me) * local, gate_rows.reshape(-1), up_rows.reshape(-1)])
        table = met(table, gate_blocks, up_blocks)
        starts = (members, members + gate_rows.size)
        run = lambda pieces, result: project(
            pieces, members * local, table, starts, blocks, result
        )

        own = Piece(tokens, [0], local, 0)
        mine = own.part(TURNED, local - TURNED)
        blocks = (gate_blocks, up_blocks)
        y1 = swap(own, "y", 0)
        z1 = swap(mine, "z", 0)
        z2 = swap(mine, "z", 1)
        y2 = swap(after(own, mine), "y", 1)
        y3 = swap(after(y1, table), "y", 1)
        z1, z2 = after(z1, y1), after(z2, y1)
        z3 = swap(z1, "z", 1)
        pair = joined(z1, z2)
        p1 = swap(after(pair, y3), "y", 0)
        column = joined(*[p.part(0, TURNED) for p in (own, y1, y2, y3)])
        b1 = swap(column, "z", 0)
        result = run([own, y1], None)
        result = run([after(y2, p1), y3, z1, z2], result)
        p2 = swap(joined(pair, p1), "y", 1)
        q1 = swap(after(z3, p1, result), "y", 0)
        b2 = swap(after(column, z3, result), "z", 1)
        b3 = swap(after(b1, q1), "z", 1)
        q2 = swap(after(joined(z3, q1), b1), "y", 1)
        for pieces in ([z3, p1, b1], [q1, p2], [b2, q2], [b3]):
            result = run(pieces, result)
        return result

    in_specs = (
        P(AXES, None),
        P("tensor", None),
        P("tensor", None, None, None),
        P("tensor", None),
        P("tensor", None, None, None),
    )
    return jax.shard_map(shards, mesh=mesh, in_specs=in_specs, out_specs=P("dp", "tensor"), check_vma=False)
```

```python
import functools

import jax
import jax.numpy as jnp
import numpy as np
from jax import lax
from jax.experimental import pallas as pl
from jax.experimental.pallas import tpu as pltpu
from jax.sharding import PartitionSpec as P

BLK = 128
SIDE = 4
AXES = ("dp", "tensor")
TURNED = 16
UNROLL = 7
COST = 30_000_000


STEPS = {("y", 0): 1, ("y", 1): 2, ("z", 0): 4, ("z", 1): 8}


def mask(core, code):
    found = 0
    for (dim, step), bit in STEPS.items():
        if code & bit:
            found ^= (1, 3)[(step + core) % 2] * (SIDE if dim == "y" else 1)
    return found


class Piece:
    def __init__(self, rows, codes, size, offset):
        self.rows, self.codes, self.size, self.offset = rows, codes, size, offset

    def part(self, offset, size):
        rows = self.rows.reshape(len(self.codes), self.size, -1)[:, offset : offset + size]
        return Piece(rows.reshape(len(self.codes) * size, -1), self.codes, size, self.offset + offset)


def joined(*pieces):
    rows = jnp.concatenate([p.rows for p in pieces], axis=0)
    return Piece(rows, sum([p.codes for p in pieces], []), pieces[0].size, pieces[0].offset)


def after(piece, *others):
    rows, *_ = lax.optimization_barrier((piece.rows, *[getattr(o, "rows", o) for o in others]))
    return Piece(rows, piece.codes, piece.size, piece.offset)


def met_kernel(table_ref, *refs):
    refs[-1][...] = table_ref[...]


def met(table, *arrays):
    vmem = pl.BlockSpec(memory_space=pltpu.VMEM)
    return pl.pallas_call(
        met_kernel,
        out_shape=jax.ShapeDtypeStruct(table.shape, table.dtype),
        in_specs=[vmem] * (1 + len(arrays)),
        out_specs=vmem,
        compiler_params=pltpu.CompilerParams(vmem_limit_bytes=1 << 20),
    )(table, *arrays)


def project_kernel(layout, starts, n_prev, table_ref, *refs):
    n = len(layout)
    pieces, (gate_ref, up_ref) = refs[:n], refs[n : n + 2]
    out_ref, hidden, sems = refs[n + 2 + n_prev :]
    columns, cap = gate_ref.shape[:2]

    def product(start, blocks_ref, c):
        listed = [table_ref[start + c * cap + j] for j in range(cap)]

        def gathered(j):
            start = pl.multiple_of(jnp.maximum(listed[j], 0) * BLK, BLK)
            return jnp.concatenate([p[:, pl.ds(start, BLK)] for p in pieces], axis=0)

        lhs = jnp.concatenate([gathered(j) for j in range(cap)], axis=1)
        rhs = jnp.concatenate(
            [jnp.where(listed[j] >= 0, blocks_ref[c, j], jnp.zeros((), blocks_ref.dtype)) for j in range(cap)], axis=0
        )
        return jnp.dot(lhs, rhs, preferred_element_type=jnp.float32)

    @pl.loop(0, columns, step=UNROLL)
    def _(first):
        for k in range(UNROLL):
            c = first + k
            gate = product(starts[0], gate_ref, c)
            up = product(starts[1], up_ref, c)
            value = gate * (1.0 / (1.0 + jnp.exp(-gate))) * up
            hidden[:, pl.ds(pl.multiple_of(c * BLK, BLK), BLK)] = value.astype(hidden.dtype)

    copies, base = [], 0
    for codes, size, offset in layout:
        for code in codes:
            i = len(copies)
            to = pl.multiple_of(table_ref[code] + offset, 16)
            copies.append(pltpu.make_async_copy(hidden.at[pl.ds(base, size)], out_ref.at[pl.ds(to, size)], sems.at[i]))
            base += size
    for copy in copies:
        copy.start()
    for copy in copies:
        copy.wait()


def project(pieces, total_rows, table, starts, blocks, result):
    rows = sum(p.rows.shape[0] for p in pieces)
    layout = [(p.codes, p.size, p.offset) for p in pieces]
    width = blocks[0].shape[0] * BLK
    prev = [] if result is None else [result]
    vmem, smem, hbm = (pl.BlockSpec(memory_space=m) for m in (pltpu.VMEM, pltpu.SMEM, pl.ANY))
    return pl.pallas_call(
        functools.partial(project_kernel, layout, starts, len(prev)),
        out_shape=jax.ShapeDtypeStruct((total_rows, width), jnp.bfloat16),
        in_specs=[smem] + [vmem] * (len(pieces) + 2) + [hbm] * len(prev),
        out_specs=hbm,
        scratch_shapes=[
            pltpu.VMEM((rows, width), jnp.bfloat16),
            pltpu.SemaphoreType.DMA((sum(len(p.codes) for p in pieces),)),
        ],
        input_output_aliases={3 + len(pieces): 0} if prev else {},
        cost_estimate=pl.CostEstimate(
            flops=COST * (rows + 110), bytes_accessed=2 * rows * width, transcendentals=rows * width
        ),
        compiler_params=pltpu.CompilerParams(vmem_limit_bytes=8 << 20),
    )(table, *[p.rows for p in pieces], *blocks, *prev)


def solution(mesh):
    groups, members = mesh.shape["dp"], mesh.shape["tensor"]

    def swap(piece, dim, step):
        bit = STEPS[dim, step]
        pairs = [(g * members + m, g * members + (m ^ mask(g % 2, bit))) for g in range(groups) for m in range(members)]
        rows = lax.ppermute(piece.rows, AXES, pairs)
        return Piece(rows, [code ^ bit for code in piece.codes], piece.size, piece.offset)

    def shards(tokens, gate_rows, gate_blocks, up_rows, up_blocks):
        local = tokens.shape[0]
        masks = jnp.asarray(np.array([[mask(core, code) for code in range(members)] for core in range(2)], np.int32))
        core, me = lax.axis_index("dp") % 2, lax.axis_index("tensor")
        table = jnp.concatenate([(masks[core] ^ me) * local, gate_rows.reshape(-1), up_rows.reshape(-1)])
        table = met(table, gate_blocks, up_blocks)
        starts = (members, members + gate_rows.size)
        run = lambda pieces, result: project(
            pieces, members * local, table, starts, blocks, result
        )

        own = Piece(tokens, [0], local, 0)
        mine = own.part(TURNED, local - TURNED)
        blocks = (gate_blocks, up_blocks)
        y1 = swap(own, "y", 0)
        z1 = swap(mine, "z", 0)
        z2 = swap(mine, "z", 1)
        y2 = swap(after(own, mine), "y", 1)
        y3 = swap(after(y1, table), "y", 1)
        result = run([after(own, y1)], None)
        z1, z2 = after(z1, y1, result), after(z2, y1, result)
        z3 = swap(z1, "z", 1)
        pair = joined(z1, z2)
        p1 = swap(after(pair, y3), "y", 0)
        column = joined(*[p.part(0, TURNED) for p in (own, y1, y2, y3)])
        b1 = swap(column, "z", 0)
        result = run([y1, after(y2, column), y3, z1, z2], result)
        p2 = swap(after(joined(pair, p1), result), "y", 1)
        q1 = swap(after(z3, p1, result), "y", 0)
        b2 = swap(after(column, z3, result), "z", 1)
        b3 = swap(after(b1, q1), "z", 1)
        q2 = swap(after(joined(z3, q1), b1), "y", 1)
        for pieces in ([z3, p1, b1], [q1, p2, b2], [q2, b3]):
            result = run(pieces, result)
        return result

    in_specs = (
        P(AXES, None),
        P("tensor", None),
        P("tensor", None, None, None),
        P("tensor", None),
        P("tensor", None, None, None),
    )
    return jax.shard_map(shards, mesh=mesh, in_specs=in_specs, out_specs=P("dp", "tensor"), check_vma=False)
```

```python
import functools

import jax
import jax.numpy as jnp
import numpy as np
from jax import lax
from jax.experimental import pallas as pl
from jax.experimental.pallas import tpu as pltpu
from jax.sharding import PartitionSpec as P

BLK = 128
SIDE = 4
AXES = ("dp", "tensor")
TURNED = 16
UNROLL = 7
COST = 30_000_000


STEPS = {("y", 0): 1, ("y", 1): 2, ("z", 0): 4, ("z", 1): 8}


def mask(core, code):
    found = 0
    for (dim, step), bit in STEPS.items():
        if code & bit:
            found ^= (1, 3)[(step + core) % 2] * (SIDE if dim == "y" else 1)
    return found


class Piece:
    def __init__(self, rows, codes, size, offset):
        self.rows, self.codes, self.size, self.offset = rows, codes, size, offset

    def part(self, offset, size):
        rows = self.rows.reshape(len(self.codes), self.size, -1)[:, offset : offset + size]
        return Piece(rows.reshape(len(self.codes) * size, -1), self.codes, size, self.offset + offset)


def joined(*pieces):
    rows = jnp.concatenate([p.rows for p in pieces], axis=0)
    return Piece(rows, sum([p.codes for p in pieces], []), pieces[0].size, pieces[0].offset)


def after(piece, *others):
    rows, *_ = lax.optimization_barrier((piece.rows, *[getattr(o, "rows", o) for o in others]))
    return Piece(rows, piece.codes, piece.size, piece.offset)


def met_kernel(table_ref, *refs):
    refs[-1][...] = table_ref[...]


def met(table, *arrays):
    vmem = pl.BlockSpec(memory_space=pltpu.VMEM)
    return pl.pallas_call(
        met_kernel,
        out_shape=jax.ShapeDtypeStruct(table.shape, table.dtype),
        in_specs=[vmem] * (1 + len(arrays)),
        out_specs=vmem,
        compiler_params=pltpu.CompilerParams(vmem_limit_bytes=1 << 20),
    )(table, *arrays)


def project_kernel(layout, starts, n_prev, table_ref, *refs):
    n = len(layout)
    pieces, (gate_ref, up_ref) = refs[:n], refs[n : n + 2]
    out_ref, hidden, sems = refs[n + 2 + n_prev :]
    columns, cap = gate_ref.shape[:2]

    def product(start, blocks_ref, c):
        listed = [table_ref[start + c * cap + j] for j in range(cap)]

        def gathered(j):
            start = pl.multiple_of(jnp.maximum(listed[j], 0) * BLK, BLK)
            return jnp.concatenate([p[:, pl.ds(start, BLK)] for p in pieces], axis=0)

        lhs = jnp.concatenate([gathered(j) for j in range(cap)], axis=1)
        rhs = jnp.concatenate(
            [jnp.where(listed[j] >= 0, blocks_ref[c, j], jnp.zeros((), blocks_ref.dtype)) for j in range(cap)], axis=0
        )
        return jnp.dot(lhs, rhs, preferred_element_type=jnp.float32)

    @pl.loop(0, columns, step=UNROLL)
    def _(first):
        for k in range(UNROLL):
            c = first + k
            gate = product(starts[0], gate_ref, c)
            up = product(starts[1], up_ref, c)
            value = gate * (1.0 / (1.0 + jnp.exp(-gate))) * up
            hidden[:, pl.ds(pl.multiple_of(c * BLK, BLK), BLK)] = value.astype(hidden.dtype)

    copies, base = [], 0
    for codes, size, offset in layout:
        for code in codes:
            i = len(copies)
            to = pl.multiple_of(table_ref[code] + offset, 16)
            copies.append(pltpu.make_async_copy(hidden.at[pl.ds(base, size)], out_ref.at[pl.ds(to, size)], sems.at[i]))
            base += size
    for copy in copies:
        copy.start()
    for copy in copies:
        copy.wait()


def project(pieces, total_rows, table, starts, blocks, result):
    rows = sum(p.rows.shape[0] for p in pieces)
    layout = [(p.codes, p.size, p.offset) for p in pieces]
    width = blocks[0].shape[0] * BLK
    prev = [] if result is None else [result]
    vmem, smem, hbm = (pl.BlockSpec(memory_space=m) for m in (pltpu.VMEM, pltpu.SMEM, pl.ANY))
    return pl.pallas_call(
        functools.partial(project_kernel, layout, starts, len(prev)),
        out_shape=jax.ShapeDtypeStruct((total_rows, width), jnp.bfloat16),
        in_specs=[smem] + [vmem] * (len(pieces) + 2) + [hbm] * len(prev),
        out_specs=hbm,
        scratch_shapes=[
            pltpu.VMEM((rows, width), jnp.bfloat16),
            pltpu.SemaphoreType.DMA((sum(len(p.codes) for p in pieces),)),
        ],
        input_output_aliases={3 + len(pieces): 0} if prev else {},
        cost_estimate=pl.CostEstimate(
            flops=COST * (rows + 110), bytes_accessed=2 * rows * width, transcendentals=rows * width
        ),
        compiler_params=pltpu.CompilerParams(vmem_limit_bytes=8 << 20),
    )(table, *[p.rows for p in pieces], *blocks, *prev)


def solution(mesh):
    groups, members = mesh.shape["dp"], mesh.shape["tensor"]

    def swap(piece, dim, step):
        bit = STEPS[dim, step]
        pairs = [(g * members + m, g * members + (m ^ mask(g % 2, bit))) for g in range(groups) for m in range(members)]
        rows = lax.ppermute(piece.rows, AXES, pairs)
        return Piece(rows, [code ^ bit for code in piece.codes], piece.size, piece.offset)

    def shards(tokens, gate_rows, gate_blocks, up_rows, up_blocks):
        local = tokens.shape[0]
        masks = jnp.asarray(np.array([[mask(core, code) for code in range(members)] for core in range(2)], np.int32))
        core, me = lax.axis_index("dp") % 2, lax.axis_index("tensor")
        table = jnp.concatenate([(masks[core] ^ me) * local, gate_rows.reshape(-1), up_rows.reshape(-1)])
        table = met(table, gate_blocks, up_blocks)
        starts = (members, members + gate_rows.size)
        run = lambda pieces, result: project(
            pieces, members * local, table, starts, blocks, result
        )

        own = Piece(tokens, [0], local, 0)
        mine = own.part(TURNED, local - TURNED)
        blocks = (gate_blocks, up_blocks)
        y1 = swap(own, "y", 0)
        z1 = swap(mine, "z", 0)
        z2 = swap(mine, "z", 1)
        y2 = swap(after(own, mine), "y", 1)
        y3 = swap(after(y1, table), "y", 1)
        result = run([after(own, y1)], None)
        z1, z2 = after(z1, y1, result), after(z2, y1, result)
        z3 = swap(z1, "z", 1)
        pair = joined(z1, z2)
        p1 = swap(after(pair, y3), "y", 0)
        column = joined(*[p.part(0, TURNED) for p in (own, y1, y2, y3)])
        b1 = swap(column, "z", 0)
        result = run([y1, after(y2, column), y3, z1, z2], result)
        p2 = swap(after(joined(pair, p1), result), "y", 1)
        q1 = swap(after(z3, p1, result), "y", 0)
        b2 = swap(after(column, z3, result), "z", 1)
        b3 = swap(after(b1, z3, result), "z", 1)
        q2 = swap(after(joined(z3, q1), b1), "y", 1)
        for pieces in ([z3, p1, b1], [q1, p2, b2], [q2, b3]):
            result = run(pieces, result)
        return result

    in_specs = (
        P(AXES, None),
        P("tensor", None),
        P("tensor", None, None, None),
        P("tensor", None),
        P("tensor", None, None, None),
    )
    return jax.shard_map(shards, mesh=mesh, in_specs=in_specs, out_specs=P("dp", "tensor"), check_vma=False)
```

```python
import functools

import jax
import jax.numpy as jnp
import numpy as np
from jax import lax
from jax.experimental import pallas as pl
from jax.experimental.pallas import tpu as pltpu
from jax.sharding import PartitionSpec as P

BLK = 128
SIDE = 4
AXES = ("dp", "tensor")
TURNED = 16
UNROLL = 7
COST = 30_000_000


STEPS = {("y", 0): 1, ("y", 1): 2, ("z", 0): 4, ("z", 1): 8}


def mask(core, code):
    found = 0
    for (dim, step), bit in STEPS.items():
        if code & bit:
            found ^= (1, 3)[(step + core) % 2] * (SIDE if dim == "y" else 1)
    return found


class Piece:
    def __init__(self, rows, codes, size, offset):
        self.rows, self.codes, self.size, self.offset = rows, codes, size, offset

    def part(self, offset, size):
        rows = self.rows.reshape(len(self.codes), self.size, -1)[:, offset : offset + size]
        return Piece(rows.reshape(len(self.codes) * size, -1), self.codes, size, self.offset + offset)


def joined(*pieces):
    rows = jnp.concatenate([p.rows for p in pieces], axis=0)
    return Piece(rows, sum([p.codes for p in pieces], []), pieces[0].size, pieces[0].offset)


def after(piece, *others):
    rows, *_ = lax.optimization_barrier((piece.rows, *[getattr(o, "rows", o) for o in others]))
    return Piece(rows, piece.codes, piece.size, piece.offset)


def met_kernel(table_ref, *refs):
    refs[-1][...] = table_ref[...]


def met(table, *arrays):
    vmem = pl.BlockSpec(memory_space=pltpu.VMEM)
    return pl.pallas_call(
        met_kernel,
        out_shape=jax.ShapeDtypeStruct(table.shape, table.dtype),
        in_specs=[vmem] * (1 + len(arrays)),
        out_specs=vmem,
        compiler_params=pltpu.CompilerParams(vmem_limit_bytes=1 << 20),
    )(table, *arrays)


def project_kernel(layout, starts, n_prev, table_ref, *refs):
    n = len(layout)
    pieces, (gate_ref, up_ref) = refs[:n], refs[n : n + 2]
    out_ref, hidden, sems = refs[n + 2 + n_prev :]
    columns, cap = gate_ref.shape[:2]

    def product(start, blocks_ref, c):
        listed = [table_ref[start + c * cap + j] for j in range(cap)]

        def gathered(j):
            start = pl.multiple_of(jnp.maximum(listed[j], 0) * BLK, BLK)
            return jnp.concatenate([p[:, pl.ds(start, BLK)] for p in pieces], axis=0)

        lhs = jnp.concatenate([gathered(j) for j in range(cap)], axis=1)
        rhs = jnp.concatenate(
            [jnp.where(listed[j] >= 0, blocks_ref[c, j], jnp.zeros((), blocks_ref.dtype)) for j in range(cap)], axis=0
        )
        return jnp.dot(lhs, rhs, preferred_element_type=jnp.float32)

    @pl.loop(0, columns, step=UNROLL)
    def _(first):
        for k in range(UNROLL):
            c = first + k
            gate = product(starts[0], gate_ref, c)
            up = product(starts[1], up_ref, c)
            value = gate * (1.0 / (1.0 + jnp.exp(-gate))) * up
            hidden[:, pl.ds(pl.multiple_of(c * BLK, BLK), BLK)] = value.astype(hidden.dtype)

    copies, base = [], 0
    for codes, size, offset in layout:
        for code in codes:
            i = len(copies)
            to = pl.multiple_of(table_ref[code] + offset, 16)
            copies.append(pltpu.make_async_copy(hidden.at[pl.ds(base, size)], out_ref.at[pl.ds(to, size)], sems.at[i]))
            base += size
    for copy in copies:
        copy.start()
    for copy in copies:
        copy.wait()


def project(pieces, total_rows, table, starts, blocks, result):
    rows = sum(p.rows.shape[0] for p in pieces)
    layout = [(p.codes, p.size, p.offset) for p in pieces]
    width = blocks[0].shape[0] * BLK
    prev = [] if result is None else [result]
    vmem, smem, hbm = (pl.BlockSpec(memory_space=m) for m in (pltpu.VMEM, pltpu.SMEM, pl.ANY))
    return pl.pallas_call(
        functools.partial(project_kernel, layout, starts, len(prev)),
        out_shape=jax.ShapeDtypeStruct((total_rows, width), jnp.bfloat16),
        in_specs=[smem] + [vmem] * (len(pieces) + 2) + [hbm] * len(prev),
        out_specs=hbm,
        scratch_shapes=[
            pltpu.VMEM((rows, width), jnp.bfloat16),
            pltpu.SemaphoreType.DMA((sum(len(p.codes) for p in pieces),)),
        ],
        input_output_aliases={3 + len(pieces): 0} if prev else {},
        cost_estimate=pl.CostEstimate(
            flops=COST * (rows + 110), bytes_accessed=2 * rows * width, transcendentals=rows * width
        ),
        compiler_params=pltpu.CompilerParams(vmem_limit_bytes=8 << 20),
    )(table, *[p.rows for p in pieces], *blocks, *prev)


def solution(mesh):
    groups, members = mesh.shape["dp"], mesh.shape["tensor"]

    def swap(piece, dim, step):
        bit = STEPS[dim, step]
        pairs = [(g * members + m, g * members + (m ^ mask(g % 2, bit))) for g in range(groups) for m in range(members)]
        rows = lax.ppermute(piece.rows, AXES, pairs)
        return Piece(rows, [code ^ bit for code in piece.codes], piece.size, piece.offset)

    def shards(tokens, gate_rows, gate_blocks, up_rows, up_blocks):
        local = tokens.shape[0]
        masks = jnp.asarray(np.array([[mask(core, code) for code in range(members)] for core in range(2)], np.int32))
        core, me = lax.axis_index("dp") % 2, lax.axis_index("tensor")
        table = jnp.concatenate([(masks[core] ^ me) * local, gate_rows.reshape(-1), up_rows.reshape(-1)])
        table = met(table, gate_blocks, up_blocks)
        starts = (members, members + gate_rows.size)
        run = lambda pieces, result: project(
            pieces, members * local, table, starts, blocks, result
        )

        own = Piece(tokens, [0], local, 0)
        mine = own.part(TURNED, local - TURNED)
        blocks = (gate_blocks, up_blocks)
        y1 = swap(own, "y", 0)
        z1 = swap(mine, "z", 0)
        z2 = swap(mine, "z", 1)
        y2 = swap(after(own, mine), "y", 1)
        y3 = swap(after(y1, table), "y", 1)
        result = run([after(own, y1)], None)
        z1, z2 = after(z1, y3, result), after(z2, y3, result)
        z3 = swap(z1, "z", 1)
        pair = joined(z1, z2)
        p1 = swap(after(pair, y3), "y", 0)
        column = joined(*[p.part(0, TURNED) for p in (own, y1, y2, y3)])
        b1 = swap(column, "z", 0)
        result = run([y1, after(y2, column), y3, z1, z2], result)
        p2 = swap(after(pair, result), "y", 1)
        p3 = swap(after(p1, result), "y", 1)
        result = run([after(p1, result)], result)
        q1 = swap(after(z3, p1, result), "y", 0)
        b2 = swap(after(column, z3, result), "z", 1)
        b3 = swap(after(b1, z3, result), "z", 1)
        q2 = swap(after(joined(z3, q1), b1), "y", 1)
        for pieces in ([z3, after(p2, q1), b1], [p3, q1, b2], [q2, b3]):
            result = run(pieces, result)
        return result

    in_specs = (
        P(AXES, None),
        P("tensor", None),
        P("tensor", None, None, None),
        P("tensor", None),
        P("tensor", None, None, None),
    )
    return jax.shard_map(shards, mesh=mesh, in_specs=in_specs, out_specs=P("dp", "tensor"), check_vma=False)
```

```python
import functools

import jax
import jax.numpy as jnp
import numpy as np
from jax import lax
from jax.experimental import pallas as pl
from jax.experimental.pallas import tpu as pltpu
from jax.sharding import PartitionSpec as P

BLK = 128
SIDE = 4
AXES = ("dp", "tensor")
TURNED = 16
UNROLL = 7
COST = 24_000_000


STEPS = {("y", 0): 1, ("y", 1): 2, ("z", 0): 4, ("z", 1): 8}


def mask(core, code):
    found = 0
    for (dim, step), bit in STEPS.items():
        if code & bit:
            found ^= (1, 3)[(step + core) % 2] * (SIDE if dim == "y" else 1)
    return found


class Piece:
    def __init__(self, rows, codes, size, offset):
        self.rows, self.codes, self.size, self.offset = rows, codes, size, offset

    def part(self, offset, size):
        rows = self.rows.reshape(len(self.codes), self.size, -1)[:, offset : offset + size]
        return Piece(rows.reshape(len(self.codes) * size, -1), self.codes, size, self.offset + offset)


def joined(*pieces):
    rows = jnp.concatenate([p.rows for p in pieces], axis=0)
    return Piece(rows, sum([p.codes for p in pieces], []), pieces[0].size, pieces[0].offset)


def after(piece, *others):
    rows, *_ = lax.optimization_barrier((piece.rows, *[getattr(o, "rows", o) for o in others]))
    return Piece(rows, piece.codes, piece.size, piece.offset)


def met_kernel(table_ref, *refs):
    refs[-1][...] = table_ref[...]


def met(table, *arrays):
    vmem = pl.BlockSpec(memory_space=pltpu.VMEM)
    return pl.pallas_call(
        met_kernel,
        out_shape=jax.ShapeDtypeStruct(table.shape, table.dtype),
        in_specs=[vmem] * (1 + len(arrays)),
        out_specs=vmem,
        compiler_params=pltpu.CompilerParams(vmem_limit_bytes=1 << 20),
    )(table, *arrays)


def project_kernel(layout, starts, n_prev, table_ref, *refs):
    n = len(layout)
    pieces, (gate_ref, up_ref) = refs[:n], refs[n : n + 2]
    out_ref, hidden, sems = refs[n + 2 + n_prev :]
    columns, cap = gate_ref.shape[:2]

    def product(start, blocks_ref, c):
        listed = [table_ref[start + c * cap + j] for j in range(cap)]

        def gathered(j):
            start = pl.multiple_of(jnp.maximum(listed[j], 0) * BLK, BLK)
            return jnp.concatenate([p[:, pl.ds(start, BLK)] for p in pieces], axis=0)

        lhs = jnp.concatenate([gathered(j) for j in range(cap)], axis=1)
        rhs = jnp.concatenate(
            [jnp.where(listed[j] >= 0, blocks_ref[c, j], jnp.zeros((), blocks_ref.dtype)) for j in range(cap)], axis=0
        )
        return jnp.dot(lhs, rhs, preferred_element_type=jnp.float32)

    @pl.loop(0, columns, step=UNROLL)
    def _(first):
        for k in range(UNROLL):
            c = first + k
            gate = product(starts[0], gate_ref, c)
            up = product(starts[1], up_ref, c)
            value = gate * (1.0 / (1.0 + jnp.exp(-gate))) * up
            hidden[:, pl.ds(pl.multiple_of(c * BLK, BLK), BLK)] = value.astype(hidden.dtype)

    copies, base = [], 0
    for codes, size, offset in layout:
        for code in codes:
            i = len(copies)
            to = pl.multiple_of(table_ref[code] + offset, 16)
            copies.append(pltpu.make_async_copy(hidden.at[pl.ds(base, size)], out_ref.at[pl.ds(to, size)], sems.at[i]))
            base += size
    for copy in copies:
        copy.start()
    for copy in copies:
        copy.wait()


def project(pieces, total_rows, table, starts, blocks, result):
    rows = sum(p.rows.shape[0] for p in pieces)
    layout = [(p.codes, p.size, p.offset) for p in pieces]
    width = blocks[0].shape[0] * BLK
    prev = [] if result is None else [result]
    vmem, smem, hbm = (pl.BlockSpec(memory_space=m) for m in (pltpu.VMEM, pltpu.SMEM, pl.ANY))
    return pl.pallas_call(
        functools.partial(project_kernel, layout, starts, len(prev)),
        out_shape=jax.ShapeDtypeStruct((total_rows, width), jnp.bfloat16),
        in_specs=[smem] + [vmem] * (len(pieces) + 2) + [hbm] * len(prev),
        out_specs=hbm,
        scratch_shapes=[
            pltpu.VMEM((rows, width), jnp.bfloat16),
            pltpu.SemaphoreType.DMA((sum(len(p.codes) for p in pieces),)),
        ],
        input_output_aliases={3 + len(pieces): 0} if prev else {},
        cost_estimate=pl.CostEstimate(
            flops=COST * (rows + 110), bytes_accessed=2 * rows * width, transcendentals=rows * width
        ),
        compiler_params=pltpu.CompilerParams(vmem_limit_bytes=8 << 20),
    )(table, *[p.rows for p in pieces], *blocks, *prev)


def solution(mesh):
    groups, members = mesh.shape["dp"], mesh.shape["tensor"]

    def swap(piece, dim, step):
        bit = STEPS[dim, step]
        pairs = [(g * members + m, g * members + (m ^ mask(g % 2, bit))) for g in range(groups) for m in range(members)]
        rows = lax.ppermute(piece.rows, AXES, pairs)
        return Piece(rows, [code ^ bit for code in piece.codes], piece.size, piece.offset)

    def shards(tokens, gate_rows, gate_blocks, up_rows, up_blocks):
        local = tokens.shape[0]
        masks = jnp.asarray(np.array([[mask(core, code) for code in range(members)] for core in range(2)], np.int32))
        core, me = lax.axis_index("dp") % 2, lax.axis_index("tensor")
        table = jnp.concatenate([(masks[core] ^ me) * local, gate_rows.reshape(-1), up_rows.reshape(-1)])
        table = met(table, gate_blocks, up_blocks)
        starts = (members, members + gate_rows.size)
        run = lambda pieces, result: project(
            pieces, members * local, table, starts, blocks, result
        )

        own = Piece(tokens, [0], local, 0)
        mine = own.part(TURNED, local - TURNED)
        blocks = (gate_blocks, up_blocks)
        y1 = swap(own, "y", 0)
        z1 = swap(mine, "z", 0)
        z2 = swap(mine, "z", 1)
        y2 = swap(after(own, mine), "y", 1)
        y3 = swap(after(y1, table), "y", 1)
        result = run([after(own, y1)], None)
        z1, z2 = after(z1, y1, result), after(z2, y1, result)
        z3 = swap(z1, "z", 1)
        pair = joined(z1, z2)
        p1 = swap(after(pair, y3), "y", 0)
        column = joined(*[p.part(0, TURNED) for p in (own, y1, y2, y3)])
        b1 = swap(column, "z", 0)
        result = run([y1, after(y2, column), y3, z1, z2], result)
        p2 = swap(after(joined(pair, p1), result), "y", 1)
        q1 = swap(after(z3, p1, result), "y", 0)
        b2 = swap(after(column, z3, result), "z", 1)
        b3 = swap(after(b1, z3, result), "z", 1)
        result = run([z3, p1, b1], result)
        q2 = swap(after(joined(z3, q1), result), "y", 1)
        for pieces in ([q1, p2, b2], [q2, b3]):
            result = run(pieces, result)
        return result

    in_specs = (
        P(AXES, None),
        P("tensor", None),
        P("tensor", None, None, None),
        P("tensor", None),
        P("tensor", None, None, None),
    )
    return jax.shard_map(shards, mesh=mesh, in_specs=in_specs, out_specs=P("dp", "tensor"), check_vma=False)
```

```python
import functools

import jax
import jax.numpy as jnp
import numpy as np
from jax import lax
from jax.experimental import pallas as pl
from jax.experimental.pallas import tpu as pltpu
from jax.sharding import PartitionSpec as P

BLK = 128
SIDE = 4
AXES = ("dp", "tensor")
TURNED = 16
UNROLL = 7
COST = 24_000_000


STEPS = {("y", 0): 1, ("y", 1): 2, ("z", 0): 4, ("z", 1): 8}


def mask(core, code):
    found = 0
    for (dim, step), bit in STEPS.items():
        if code & bit:
            found ^= (1, 3)[(step + core) % 2] * (SIDE if dim == "y" else 1)
    return found


class Piece:
    def __init__(self, rows, codes, size, offset):
        self.rows, self.codes, self.size, self.offset = rows, codes, size, offset

    def part(self, offset, size):
        rows = self.rows.reshape(len(self.codes), self.size, -1)[:, offset : offset + size]
        return Piece(rows.reshape(len(self.codes) * size, -1), self.codes, size, self.offset + offset)


def joined(*pieces):
    rows = jnp.concatenate([p.rows for p in pieces], axis=0)
    return Piece(rows, sum([p.codes for p in pieces], []), pieces[0].size, pieces[0].offset)


def after(piece, *others):
    rows, *_ = lax.optimization_barrier((piece.rows, *[getattr(o, "rows", o) for o in others]))
    return Piece(rows, piece.codes, piece.size, piece.offset)


def met_kernel(table_ref, *refs):
    refs[-1][...] = table_ref[...]


def met(table, *arrays):
    vmem = pl.BlockSpec(memory_space=pltpu.VMEM)
    return pl.pallas_call(
        met_kernel,
        out_shape=jax.ShapeDtypeStruct(table.shape, table.dtype),
        in_specs=[vmem] * (1 + len(arrays)),
        out_specs=vmem,
        compiler_params=pltpu.CompilerParams(vmem_limit_bytes=1 << 20),
    )(table, *arrays)


def project_kernel(layout, starts, n_prev, table_ref, *refs):
    n = len(layout)
    pieces, (gate_ref, up_ref) = refs[:n], refs[n : n + 2]
    out_ref, hidden, sems = refs[n + 2 + n_prev :]
    columns, cap = gate_ref.shape[:2]

    def product(start, blocks_ref, c):
        listed = [table_ref[start + c * cap + j] for j in range(cap)]

        def gathered(j):
            start = pl.multiple_of(jnp.maximum(listed[j], 0) * BLK, BLK)
            return jnp.concatenate([p[:, pl.ds(start, BLK)] for p in pieces], axis=0)

        lhs = jnp.concatenate([gathered(j) for j in range(cap)], axis=1)
        rhs = jnp.concatenate(
            [jnp.where(listed[j] >= 0, blocks_ref[c, j], jnp.zeros((), blocks_ref.dtype)) for j in range(cap)], axis=0
        )
        return jnp.dot(lhs, rhs, preferred_element_type=jnp.float32)

    @pl.loop(0, columns, step=UNROLL)
    def _(first):
        for k in range(UNROLL):
            c = first + k
            gate = product(starts[0], gate_ref, c)
            up = product(starts[1], up_ref, c)
            value = gate * (1.0 / (1.0 + jnp.exp(-gate))) * up
            hidden[:, pl.ds(pl.multiple_of(c * BLK, BLK), BLK)] = value.astype(hidden.dtype)

    copies, base = [], 0
    for codes, size, offset in layout:
        for code in codes:
            i = len(copies)
            to = pl.multiple_of(table_ref[code] + offset, 16)
            copies.append(pltpu.make_async_copy(hidden.at[pl.ds(base, size)], out_ref.at[pl.ds(to, size)], sems.at[i]))
            base += size
    for copy in copies:
        copy.start()
    for copy in copies:
        copy.wait()


def project(pieces, total_rows, table, starts, blocks, result):
    rows = sum(p.rows.shape[0] for p in pieces)
    layout = [(p.codes, p.size, p.offset) for p in pieces]
    width = blocks[0].shape[0] * BLK
    prev = [] if result is None else [result]
    vmem, smem, hbm = (pl.BlockSpec(memory_space=m) for m in (pltpu.VMEM, pltpu.SMEM, pl.ANY))
    return pl.pallas_call(
        functools.partial(project_kernel, layout, starts, len(prev)),
        out_shape=jax.ShapeDtypeStruct((total_rows, width), jnp.bfloat16),
        in_specs=[smem] + [vmem] * (len(pieces) + 2) + [hbm] * len(prev),
        out_specs=hbm,
        scratch_shapes=[
            pltpu.VMEM((rows, width), jnp.bfloat16),
            pltpu.SemaphoreType.DMA((sum(len(p.codes) for p in pieces),)),
        ],
        input_output_aliases={3 + len(pieces): 0} if prev else {},
        cost_estimate=pl.CostEstimate(
            flops=COST * (rows + 110), bytes_accessed=2 * rows * width, transcendentals=rows * width
        ),
        compiler_params=pltpu.CompilerParams(vmem_limit_bytes=8 << 20),
    )(table, *[p.rows for p in pieces], *blocks, *prev)


def solution(mesh):
    groups, members = mesh.shape["dp"], mesh.shape["tensor"]

    def swap(piece, dim, step):
        bit = STEPS[dim, step]
        pairs = [(g * members + m, g * members + (m ^ mask(g % 2, bit))) for g in range(groups) for m in range(members)]
        rows = lax.ppermute(piece.rows, AXES, pairs)
        return Piece(rows, [code ^ bit for code in piece.codes], piece.size, piece.offset)

    def shards(tokens, gate_rows, gate_blocks, up_rows, up_blocks):
        local = tokens.shape[0]
        masks = jnp.asarray(np.array([[mask(core, code) for code in range(members)] for core in range(2)], np.int32))
        core, me = lax.axis_index("dp") % 2, lax.axis_index("tensor")
        table = jnp.concatenate([(masks[core] ^ me) * local, gate_rows.reshape(-1), up_rows.reshape(-1)])
        table = met(table, gate_blocks, up_blocks)
        starts = (members, members + gate_rows.size)
        run = lambda pieces, result: project(
            pieces, members * local, table, starts, blocks, result
        )

        own = Piece(tokens, [0], local, 0)
        mine = own.part(TURNED, local - TURNED)
        blocks = (gate_blocks, up_blocks)
        y1 = swap(own, "y", 0)
        z1 = swap(mine, "z", 0)
        z2 = swap(mine, "z", 1)
        y2 = swap(after(own, mine), "y", 1)
        y3 = swap(after(y1, table), "y", 1)
        result = run([after(own, y1)], None)
        z1, z2 = after(z1, y1, result), after(z2, y1, result)
        z3 = swap(z1, "z", 1)
        pair = joined(z1, z2)
        p1 = swap(after(pair, y3), "y", 0)
        column = joined(*[p.part(0, TURNED) for p in (own, y1, y2, y3)])
        b1 = swap(column, "z", 0)
        result = run([y1, after(y2, column), y3, z1, z2], result)
        p2 = swap(after(joined(pair, p1), result), "y", 1)
        q1 = swap(after(z3, p1, result), "y", 0)
        b2 = swap(after(column, z3, result), "z", 1)
        b3 = swap(after(b1, q1), "z", 1)
        result = run([z3, p1, b1], result)
        q2 = swap(after(joined(z3, q1), result), "y", 1)
        for pieces in ([q1, p2, b2], [q2, b3]):
            result = run(pieces, result)
        return result

    in_specs = (
        P(AXES, None),
        P("tensor", None),
        P("tensor", None, None, None),
        P("tensor", None),
        P("tensor", None, None, None),
    )
    return jax.shard_map(shards, mesh=mesh, in_specs=in_specs, out_specs=P("dp", "tensor"), check_vma=False)
```

```python
import functools

import jax
import jax.numpy as jnp
import numpy as np
from jax import lax
from jax.experimental import pallas as pl
from jax.experimental.pallas import tpu as pltpu
from jax.sharding import PartitionSpec as P

BLK = 128
SIDE = 4
AXES = ("dp", "tensor")
TURNED = 16
UNROLL = 7
COST = 24_000_000


STEPS = {("y", 0): 1, ("y", 1): 2, ("z", 0): 4, ("z", 1): 8}


def mask(core, code):
    found = 0
    for (dim, step), bit in STEPS.items():
        if code & bit:
            found ^= (1, 3)[(step + core) % 2] * (SIDE if dim == "y" else 1)
    return found


class Piece:
    def __init__(self, rows, codes, size, offset):
        self.rows, self.codes, self.size, self.offset = rows, codes, size, offset

    def part(self, offset, size):
        rows = self.rows.reshape(len(self.codes), self.size, -1)[:, offset : offset + size]
        return Piece(rows.reshape(len(self.codes) * size, -1), self.codes, size, self.offset + offset)


def joined(*pieces):
    rows = jnp.concatenate([p.rows for p in pieces], axis=0)
    return Piece(rows, sum([p.codes for p in pieces], []), pieces[0].size, pieces[0].offset)


def after(piece, *others):
    rows, *_ = lax.optimization_barrier((piece.rows, *[getattr(o, "rows", o) for o in others]))
    return Piece(rows, piece.codes, piece.size, piece.offset)


def met_kernel(table_ref, *refs):
    refs[-1][...] = table_ref[...]


def met(table, *arrays):
    vmem = pl.BlockSpec(memory_space=pltpu.VMEM)
    return pl.pallas_call(
        met_kernel,
        out_shape=jax.ShapeDtypeStruct(table.shape, table.dtype),
        in_specs=[vmem] * (1 + len(arrays)),
        out_specs=vmem,
        compiler_params=pltpu.CompilerParams(vmem_limit_bytes=1 << 20),
    )(table, *arrays)


def project_kernel(layout, starts, n_prev, table_ref, *refs):
    n = len(layout)
    pieces, (gate_ref, up_ref) = refs[:n], refs[n : n + 2]
    out_ref, hidden, sems = refs[n + 2 + n_prev :]
    columns, cap = gate_ref.shape[:2]

    def product(start, blocks_ref, c):
        listed = [table_ref[start + c * cap + j] for j in range(cap)]

        def gathered(j):
            start = pl.multiple_of(jnp.maximum(listed[j], 0) * BLK, BLK)
            return jnp.concatenate([p[:, pl.ds(start, BLK)] for p in pieces], axis=0)

        lhs = jnp.concatenate([gathered(j) for j in range(cap)], axis=1)
        rhs = jnp.concatenate(
            [jnp.where(listed[j] >= 0, blocks_ref[c, j], jnp.zeros((), blocks_ref.dtype)) for j in range(cap)], axis=0
        )
        return jnp.dot(lhs, rhs, preferred_element_type=jnp.float32)

    @pl.loop(0, columns, step=UNROLL)
    def _(first):
        for k in range(UNROLL):
            c = first + k
            gate = product(starts[0], gate_ref, c)
            up = product(starts[1], up_ref, c)
            value = gate * (1.0 / (1.0 + jnp.exp(-gate))) * up
            hidden[:, pl.ds(pl.multiple_of(c * BLK, BLK), BLK)] = value.astype(hidden.dtype)

    copies, base = [], 0
    for codes, size, offset in layout:
        for code in codes:
            i = len(copies)
            to = pl.multiple_of(table_ref[code] + offset, 16)
            copies.append(pltpu.make_async_copy(hidden.at[pl.ds(base, size)], out_ref.at[pl.ds(to, size)], sems.at[i]))
            base += size
    for copy in copies:
        copy.start()
    for copy in copies:
        copy.wait()


def project(pieces, total_rows, table, starts, blocks, result):
    rows = sum(p.rows.shape[0] for p in pieces)
    layout = [(p.codes, p.size, p.offset) for p in pieces]
    width = blocks[0].shape[0] * BLK
    prev = [] if result is None else [result]
    vmem, smem, hbm = (pl.BlockSpec(memory_space=m) for m in (pltpu.VMEM, pltpu.SMEM, pl.ANY))
    return pl.pallas_call(
        functools.partial(project_kernel, layout, starts, len(prev)),
        out_shape=jax.ShapeDtypeStruct((total_rows, width), jnp.bfloat16),
        in_specs=[smem] + [vmem] * (len(pieces) + 2) + [hbm] * len(prev),
        out_specs=hbm,
        scratch_shapes=[
            pltpu.VMEM((rows, width), jnp.bfloat16),
            pltpu.SemaphoreType.DMA((sum(len(p.codes) for p in pieces),)),
        ],
        input_output_aliases={3 + len(pieces): 0} if prev else {},
        cost_estimate=pl.CostEstimate(
            flops=COST * (rows + 110), bytes_accessed=2 * rows * width, transcendentals=rows * width
        ),
        compiler_params=pltpu.CompilerParams(vmem_limit_bytes=8 << 20),
    )(table, *[p.rows for p in pieces], *blocks, *prev)


def solution(mesh):
    groups, members = mesh.shape["dp"], mesh.shape["tensor"]

    def swap(piece, dim, step):
        bit = STEPS[dim, step]
        pairs = [(g * members + m, g * members + (m ^ mask(g % 2, bit))) for g in range(groups) for m in range(members)]
        rows = lax.ppermute(piece.rows, AXES, pairs)
        return Piece(rows, [code ^ bit for code in piece.codes], piece.size, piece.offset)

    def shards(tokens, gate_rows, gate_blocks, up_rows, up_blocks):
        local = tokens.shape[0]
        masks = jnp.asarray(np.array([[mask(core, code) for code in range(members)] for core in range(2)], np.int32))
        core, me = lax.axis_index("dp") % 2, lax.axis_index("tensor")
        table = jnp.concatenate([(masks[core] ^ me) * local, gate_rows.reshape(-1), up_rows.reshape(-1)])
        table = met(table, gate_blocks, up_blocks)
        starts = (members, members + gate_rows.size)
        run = lambda pieces, result: project(
            pieces, members * local, table, starts, blocks, result
        )

        own = Piece(tokens, [0], local, 0)
        mine = own.part(TURNED, local - TURNED)
        blocks = (gate_blocks, up_blocks)
        y1 = swap(own, "y", 0)
        z1 = swap(mine, "z", 0)
        z2 = swap(mine, "z", 1)
        y2 = swap(after(own, mine), "y", 1)
        y3 = swap(after(y1, table), "y", 1)
        result = run([after(own, y1)], None)
        z1, z2 = after(z1, y1, result), after(z2, y1, result)
        z3 = swap(z1, "z", 1)
        pair = joined(z1, z2)
        p1 = swap(after(pair, y3), "y", 0)
        column = joined(*[p.part(0, TURNED) for p in (own, y1, y2, y3)])
        b1 = swap(column, "z", 0)
        result = run([y1, after(y2, column), y3, z1, z2], result)
        p2 = swap(after(joined(pair, p1), result), "y", 1)
        q1 = swap(after(z3, p1, result), "y", 0)
        b2 = swap(after(column, z3, result), "z", 1)
        b3 = swap(after(b1, q1), "z", 1)
        result = run([z3, p1, b1], result)
        q2 = swap(after(joined(z3, q1), p2, result), "y", 1)
        for pieces in ([q1, p2, b2], [q2, b3]):
            result = run(pieces, result)
        return result

    in_specs = (
        P(AXES, None),
        P("tensor", None),
        P("tensor", None, None, None),
        P("tensor", None),
        P("tensor", None, None, None),
    )
    return jax.shard_map(shards, mesh=mesh, in_specs=in_specs, out_specs=P("dp", "tensor"), check_vma=False)
```
